256 devices in a mesh: lat: 4 (over x), lon: 32 (over y, z_hi, core), feat: 2 (over z_lo).
Axes of the slice: x: 4, y: 4, z: 8 (z_hi: 4, z_lo: 2; z = z_hi * 2 + z_lo), core: 2. Of those that a mesh axis runs over, the one named last changes fastest.
Arguments:
- atmosphere: float32 [384, 768, 256], P('lat', 'lon', 'feat'), may hold values from -6 to 6
- spectral_weight: float32 [2, 384, 256, 256], P(None, ('lat', 'lon'), None, 'feat'), may hold values from -0.25 to 0.25
- mlp_in: float32 [256, 768], P(None, 'feat'), may hold values from -0.375 to 0.375
- mlp_out: float32 [768, 256], P(None, 'feat'), may hold values from -0.21875 to 0.21875
- ocean_state: float32 [256, 512, 256], P('lat', 'lon', 'feat'), may hold values from -6 to 6
- depth_kernel: float32 [7, 7, 256], P(None, None, 'feat'), may hold values from -0.875 to 0.875
- depth_bias: float32 [256], P('feat'), may hold values from -4 to 4
- norm_gain: float32 [256], replicated, may hold values from 0.5 to 1.5
- ocean_up: float32 [256, 1024], P(None, 'feat'), may hold values from -0.375 to 0.375
- ocean_down: float32 [1024, 256], P(None, 'feat'), may hold values from -0.1875 to 0.1875
- ocean_bias: float32 [256], P('feat'), may hold values from -3 to 3
- layer_scale: float32 [256], P('feat'), may hold values from 0.5 to 1.5
- flux_weight: float32 [256, 256], P(None, 'feat'), may hold values from -0.375 to 0.375
- regrid_rows: int32 [4, 32, 32, 32], P('lat', 'lon'), may hold values from 0 to 2303
- ocean_rows: int32 [256, 512], P('lat', 'lon'), may hold values from 0 to 1023
- land_mask: int32 [32, 64], P('lat', 'lon'), may hold values 0 or 1
Outputs:
- atmos_next: float32 [384, 768, 256], P('lat', 'lon', 'feat')
- ocean_next: float32 [256, 512, 256], P('lat', 'lon', 'feat')
The draws below stay inside these ranges and needn't reach their ends.
Inputs may be any that keep to these rules, and one draw needn't show every extreme that they name: regrid_rows[a, s, b, k] counts the points of latitude band a and longitude sector s latitude-major, 24 to a latitude. ocean_rows[i, o] = s * 32 + k names the k-th point that the cell's tile takes from sector s. `land_mask`: 1 for a sea block, 0 for a land block.
All inputs are finite; a program needn't handle non-finite values.
Results may differ from the reference program's by a relative error of at most 0.0003.
Values sent between devices are 32-bit elements; how exact they have to be, the bound alone decides.
No kernel may reach another device: no remote copies, remote signals or barrier semaphores. Data moves between devices by JAX's collectives and lax.ppermute only.
A program may use at most 128 MiB of HBM per device.

```python
import math
import jax
import jax.numpy as jnp
from jax import lax

C = 256
HID = 768
NLAT = 384
NLON = 768
LMAX = 384
MMAX = 256
CO = 256
HO = 1024
KERNEL = 7
BLOCK = 8
OLAT = 256
OLON = 512
PICKS = 32
ATM_ROWS = 2304
N_LAT = 4
N_LON = 32


def set_ends(values, rng, least, largest):
    dims = values.shape
    spot = [jax.random.randint(jax.random.fold_in(rng, axis), (), 0, dims[axis]) for axis in range(len(dims))]
    values = values.at[tuple(spot)].set(least)
    longest = dims.index(max(dims))
    spot[longest] = (spot[longest] + 1) % dims[longest]
    return values.at[tuple(spot)].set(largest)


def levels(stream_key, extent, shards, low, high):
    def one(axis_at, blocks):
        draws = jax.random.uniform(jax.random.fold_in(jax.random.fold_in(stream_key, 6), axis_at), (blocks,), jnp.float32, low / len(shards), high / len(shards))
        return jnp.repeat(jnp.exp(draws), extent[axis_at] // blocks).reshape((-1,) + (1,) * (len(extent) - axis_at - 1))

    loudness = one(*shards[0])
    for cut in shards[1:]:
        loudness = loudness * one(*cut)
    return loudness


def gaussian(own_key, extent, spread, reach, split=(), kind=jnp.bfloat16):
    array = spread * jax.random.normal(own_key, extent, jnp.float32)
    if split:
        array = array * levels(own_key, extent, split, -0.22, 0.18)
    return jnp.clip(array, -reach, reach).astype(kind)


def setup_inputs(seed: int = 0) -> dict:
    arg_keys = jax.random.split(jax.random.key(seed), 17)
    return {
        "atmosphere": gaussian(arg_keys[0], (NLAT, NLON, C), 1.0, 6.0, ((0, 4), (1, 32), (2, 2)), jnp.float32),
        "spectral_weight": gaussian(arg_keys[1], (2, LMAX, C, C), (2 * C) ** -0.5, 0.25, ((1, 128), (3, 2)), jnp.float32),
        "mlp_in": gaussian(arg_keys[2], (C, HID), C ** -0.5, 0.375, ((1, 2),), jnp.float32),
        "mlp_out": gaussian(arg_keys[3], (HID, C), HID ** -0.5, 0.21875, ((1, 2),), jnp.float32),
        "ocean_state": gaussian(arg_keys[4], (OLAT, OLON, CO), 1.0, 6.0, ((0, 4), (1, 32), (2, 2)), jnp.float32),
        "depth_kernel": gaussian(arg_keys[5], (KERNEL, KERNEL, CO), (KERNEL * KERNEL) ** -0.5, 0.875, ((2, 2),), jnp.float32),
        "depth_bias": gaussian(arg_keys[6], (CO,), 0.7, 4.0, ((0, 2),), jnp.float32),
        "norm_gain": jnp.clip(jax.random.uniform(arg_keys[7], (CO,), jnp.float32, 0.5, 1.5), 0.5, 1.5),
        "ocean_up": gaussian(arg_keys[8], (CO, HO), CO ** -0.5, 0.375, ((1, 2),), jnp.float32),
        "ocean_down": gaussian(arg_keys[9], (HO, CO), HO ** -0.5, 0.1875, ((1, 2),), jnp.float32),
        "ocean_bias": gaussian(arg_keys[10], (CO,), 0.5, 3.0, ((0, 2),), jnp.float32),
        "layer_scale": jnp.clip(0.5 + 1.0 * jax.random.uniform(arg_keys[11], (CO,), jnp.float32) ** levels(arg_keys[11], (CO,), ((0, 2),), -0.2, 0.2), 0.5, 1.5),
        "flux_weight": gaussian(arg_keys[12], (C, CO), C ** -0.5, 0.375, ((1, 2),), jnp.float32),
        "regrid_rows": set_ends(jax.random.randint(arg_keys[13], (N_LAT, N_LON, N_LON, PICKS), 0, ATM_ROWS), jax.random.fold_in(arg_keys[13], 1), 0, ATM_ROWS - 1).astype(jnp.int32),
        "ocean_rows": set_ends(jax.random.randint(arg_keys[14], (OLAT, OLON), 0, N_LON * PICKS), jax.random.fold_in(arg_keys[14], 1), 0, (N_LON * PICKS) - 1).astype(jnp.int32),
        "land_mask": set_ends((jax.random.randint(arg_keys[15], (OLAT // BLOCK, OLON // BLOCK), 0, 4) < 3).astype(jnp.int32), jax.random.fold_in(arg_keys[15], 1), 0, 1),
    }


best_precision = lax.Precision.HIGHEST

def legendre_table(orders, degree_count, lat_count, order_limit):
    index_lat = jnp.arange(lat_count, dtype=jnp.int32).astype(jnp.float32)
    colat = math.pi * (index_lat + 0.5) / lat_count
    cosine = jnp.cos(colat)
    sine = jnp.sin(colat)
    order_f = orders.astype(jnp.float32)[:, None]
    steps_k = jnp.arange(1, order_limit + 1, dtype=jnp.int32)
    step_f = steps_k.astype(jnp.float32)
    log_terms = jnp.log((2.0 * step_f + 1.0) / (2.0 * step_f))
    log_norm = lax.optimization_barrier(jnp.sum(jnp.where(steps_k[None, :] <= orders[:, None], log_terms[None, :], 0.0), axis=1))
    log_start = 0.5 * (math.log(0.5) + log_norm[:, None]) + order_f * jnp.log(sine)[None, :]
    zeros_grid = jnp.zeros((orders.shape[0], lat_count), jnp.float32)

    def advance(carry, degree):
        current, previous, shift = carry
        deg_f = degree.astype(jnp.float32)
        order_sq = order_f * order_f
        factor_a = jnp.sqrt(jnp.maximum(4.0 * deg_f * deg_f - 1.0, 0.0) / jnp.maximum(deg_f * deg_f - order_sq, 1.0))
        below = deg_f - 1.0
        factor_b = jnp.sqrt(jnp.maximum(below * below - order_sq, 0.0) / jnp.maximum(4.0 * below * below - 1.0, 1.0))
        recurred = factor_a * (cosine[None, :] * current - factor_b * previous)
        fresh = jnp.where(degree == orders[:, None], 1.0, jnp.where(degree > orders[:, None], recurred, 0.0))
        large = jnp.abs(fresh) > 2.0 ** 32
        rescale = jnp.where(large, 2.0 ** (-32), 1.0)
        fresh = fresh * rescale
        shift = shift + jnp.where(large, 32.0, 0.0)
        value = fresh * jnp.exp(log_start + shift * math.log(2.0))
        return ((fresh, current * rescale, shift), value)
    final_state, table = lax.scan(advance, (zeros_grid, zeros_grid, zeros_grid), jnp.arange(degree_count, dtype=jnp.int32), unroll=16)
    return table

def quadrature(lat_ids, lat_count):
    colat = math.pi * (lat_ids.astype(jnp.float32) + 0.5) / lat_count
    return jnp.sin(colat) * (math.pi / lat_count)

def forward_table(lon_count, order_count):
    lon_ids = jnp.arange(lon_count, dtype=jnp.int32)[:, None]
    order_ids = jnp.arange(order_count, dtype=jnp.int32)[None, :]
    phase = 2.0 * math.pi / lon_count * (lon_ids * order_ids % lon_count).astype(jnp.float32)
    return jnp.stack([jnp.cos(phase), -jnp.sin(phase)], axis=0) / lon_count

def inverse_table(lon_count, order_count):
    order_ids = jnp.arange(order_count, dtype=jnp.int32)[:, None]
    lon_ids = jnp.arange(lon_count, dtype=jnp.int32)[None, :]
    phase = 2.0 * math.pi / lon_count * (order_ids * lon_ids % lon_count).astype(jnp.float32)
    weight = jnp.where(order_ids == 0, 1.0, 2.0)
    return jnp.stack([jnp.cos(phase) * weight, -jnp.sin(phase) * weight], axis=0)

def reference(atmosphere, spectral_weight, mlp_in, mlp_out, ocean_state, depth_kernel, depth_bias, norm_gain, ocean_up, ocean_down, ocean_bias, layer_scale, flux_weight, regrid_rows, ocean_rows, land_mask):
    lat_ids = jnp.arange(NLAT, dtype=jnp.int32)
    table = legendre_table(jnp.arange(MMAX, dtype=jnp.int32), LMAX, NLAT, MMAX)
    quad = quadrature(lat_ids, NLAT)
    modes = jnp.einsum('jnc,rnm->mrjc', atmosphere, forward_table(NLON, MMAX), precision=best_precision)
    coeffs = jnp.einsum('lmj,mrjc->lrmc', table * quad[None, None, :], modes, precision=best_precision)
    real_part = jnp.einsum('lmc,lcd->lmd', coeffs[:, 0], spectral_weight[0], precision=best_precision) - jnp.einsum('lmc,lcd->lmd', coeffs[:, 1], spectral_weight[1], precision=best_precision)
    imag_part = jnp.einsum('lmc,lcd->lmd', coeffs[:, 1], spectral_weight[0], precision=best_precision) + jnp.einsum('lmc,lcd->lmd', coeffs[:, 0], spectral_weight[1], precision=best_precision)
    mixed = jnp.stack([real_part, imag_part], axis=1)
    grid_modes = jnp.einsum('lmj,lrmc->jrmc', table, mixed, precision=best_precision)
    spectral_field = jnp.einsum('jrmc,rmn->jnc', grid_modes, inverse_table(NLON, MMAX), precision=best_precision)
    summed = atmosphere + spectral_field

    def row_block(rows):
        hidden = jax.nn.gelu(jnp.dot(rows, mlp_in, precision=best_precision, preferred_element_type=jnp.float32), approximate=False)
        return rows + jnp.dot(hidden, mlp_out, precision=best_precision, preferred_element_type=jnp.float32)
    atmos_next = lax.map(row_block, summed)
    row_ids = jnp.arange(OLAT, dtype=jnp.int32)[:, None]
    col_ids = jnp.arange(OLON, dtype=jnp.int32)[None, :]
    band = jnp.broadcast_to(row_ids // (OLAT // N_LAT), (OLAT, OLON))
    tile = jnp.broadcast_to(col_ids // (OLON // N_LON), (OLAT, OLON))
    sector = ocean_rows // PICKS
    slot_ids = ocean_rows % PICKS
    local_ids = regrid_rows[band, sector, tile, slot_ids]
    atm_lat = NLAT // N_LAT
    atm_lon = NLON // N_LON
    lat_pick = band * atm_lat + local_ids // atm_lon
    lon_pick = sector * atm_lon + local_ids % atm_lon
    picked = atmosphere[lat_pick, lon_pick]
    forcing = jnp.dot(picked.reshape(-1, C), flux_weight, precision=best_precision, preferred_element_type=jnp.float32).reshape(OLAT, OLON, CO)
    half_side = KERNEL // 2
    padded = jnp.pad(ocean_state, ((half_side, half_side), (half_side, half_side), (0, 0)))
    conv = jnp.zeros((OLAT, OLON, CO), jnp.float32) + depth_bias
    for tap_row in range(KERNEL):
        for tap_col in range(KERNEL):
            conv = conv + padded[tap_row:tap_row + OLAT, tap_col:tap_col + OLON] * depth_kernel[tap_row, tap_col]
    joined = conv + forcing
    row_mean = lax.optimization_barrier(jnp.mean(joined, axis=-1, keepdims=True))
    centered = joined - row_mean
    variance = lax.optimization_barrier(jnp.mean(centered * centered, axis=-1, keepdims=True))
    normed = centered * lax.rsqrt(variance + 1e-06) * norm_gain
    ocean_hidden = jax.nn.gelu(jnp.dot(normed.reshape(-1, CO), ocean_up, precision=best_precision, preferred_element_type=jnp.float32), approximate=False)
    update = (jnp.dot(ocean_hidden, ocean_down, precision=best_precision, preferred_element_type=jnp.float32) + ocean_bias).reshape(OLAT, OLON, CO)
    cell_mask = jnp.broadcast_to(land_mask[:, None, :, None], (OLAT // BLOCK, BLOCK, OLON // BLOCK, BLOCK)).reshape(OLAT, OLON).astype(jnp.float32)
    ocean_next = ocean_state + cell_mask[:, :, None] * layer_scale * update
    return (atmos_next, ocean_next)
```

```python
import functools
import math

import jax
import jax.numpy as jnp
from jax import lax
from jax.experimental import pallas as pl
from jax.experimental.pallas import tpu as pltpu
from jax.sharding import Mesh, PartitionSpec as P

C = 256
NLAT = 384
NLON = 768
LMAX = 384
MMAX = 256
KERNEL = 7
BLOCK = 8

LON = ("y", "zh", "core")
ORDER_AXES = ("lat", "y", "core")
CHAN_AXES = ("zh", "feat")
F32 = jnp.float32
BF16 = jnp.bfloat16
high = lax.Precision.HIGH


def split(value):
    upper = value.astype(BF16)
    return upper, (value - upper.astype(F32)).astype(BF16)


def mm(left, right):
    return jnp.dot(left, right, preferred_element_type=F32)


def dot3(left, right):
    return mm(left[0], right[0]) + (mm(left[0], right[1]) + mm(left[1], right[0]))


def pack(pieces):
    place = lax.broadcasted_iota(jnp.int32, pieces[0][0].shape, 1) // 32
    out = None
    for i, (tile, chunk) in enumerate(pieces):
        shift = (32 * (i - chunk)) % 128
        moved = tile if shift == 0 else pltpu.roll(tile, shift, 1)
        out = moved if out is None else jnp.where(place == i, moved, out)
    return out


def local_call(kernel, out_shape, scratch=(), name=None, smem=0):
    def run(*args):
        specs = [pl.BlockSpec(memory_space=pltpu.SMEM)] * smem
        specs += [pl.BlockSpec(memory_space=pltpu.VMEM)] * (len(args) - smem)
        return pl.pallas_call(
            kernel,
            out_shape=out_shape,
            in_specs=specs,
            out_specs=jax.tree.map(lambda _: pl.BlockSpec(memory_space=pltpu.VMEM), out_shape),
            scratch_shapes=list(scratch),
            name=name,
        )(*args)

    return run


def shape(*dims, dtype=F32):
    return jax.ShapeDtypeStruct(dims, dtype)


def table_kernel(order_ref, start_ref, cos_ref, quad_ref, fh_ref, fl_ref, ih_ref, il_ref, rows_ref):
    order = order_ref[...]
    order_sq = order * order
    cosine = jnp.broadcast_to(cos_ref[...], order.shape)
    start = start_ref[...]

    def six(group, carry):
        current, previous, shift = carry
        for off in range(6):
            deg = jnp.full(order.shape, group * 6 + off, jnp.int32).astype(F32)
            factor_a = jnp.sqrt(
                jnp.maximum(4.0 * deg * deg - 1.0, 0.0) / jnp.maximum(deg * deg - order_sq, 1.0)
            )
            below = deg - 1.0
            factor_b = jnp.sqrt(
                jnp.maximum(below * below - order_sq, 0.0)
                / jnp.maximum(4.0 * below * below - 1.0, 1.0)
            )
            recurred = factor_a * (cosine * current - factor_b * previous)
            fresh = jnp.where(deg == order, 1.0, jnp.where(deg > order, recurred, 0.0))
            large = jnp.abs(fresh) > 2.0**32
            rescale = jnp.where(large, 2.0 ** (-32), 1.0)
            fresh = fresh * rescale
            shift = shift + jnp.where(large, 32.0, 0.0)
            value = fresh * jnp.exp(start + shift * math.log(2.0))
            pos = (off % 2) * 192 + (group % 4) * 48 + (off // 2) * 16 + group // 4
            where = pl.ds(pl.multiple_of(pos * 8, 8), 8)
            rows_ref[0, where, :] = value[:, :128]
            rows_ref[1, where, :] = value[:, 128:]
            previous = current * rescale
            current = fresh
        return current, previous, shift

    zeros = jnp.zeros(order.shape, F32)
    lax.fori_loop(0, LMAX // 6, six, (zeros, zeros, zeros))
    quad = quad_ref[...]
    for m in range(8):
        for parity in range(2):
            part = jnp.concatenate(
                [rows_ref[g, pl.ds(parity * 1536 + m, 192, stride=8), :] for g in range(2)], axis=1
            )
            upper, lower = split(part * quad)
            fh_ref[m, parity] = upper[:, :192]
            fl_ref[m, parity] = lower[:, :192]
            turned = jnp.transpose(part)[:192]
            upper, lower = split(turned)
            ih_ref[m, parity] = upper
            il_ref[m, parity] = lower


def legendre_tables(orders):
    column = jnp.arange(256, dtype=jnp.int32)
    lat_id = jnp.where(column < 192, 12 * (column % 16) + column // 16, 0).astype(F32)
    colat = math.pi * (lat_id + 0.5) / NLAT
    sine = jnp.sin(colat)
    order_f = orders.astype(F32)[:, None]
    steps_k = jnp.arange(1, MMAX + 1, dtype=jnp.int32)
    step_f = steps_k.astype(F32)
    log_terms = jnp.log((2.0 * step_f + 1.0) / (2.0 * step_f))
    log_norm = jnp.sum(
        jnp.where(steps_k[None, :] <= orders[:, None], log_terms[None, :], 0.0), axis=1
    )
    log_start = 0.5 * (math.log(0.5) + log_norm[:, None]) + order_f * jnp.log(sine)[None, :]
    return local_call(
        table_kernel,
        (
            shape(8, 2, 192, 192, dtype=BF16),
            shape(8, 2, 192, 192, dtype=BF16),
            shape(8, 2, 192, 192, dtype=BF16),
            shape(8, 2, 192, 192, dtype=BF16),
        ),
        scratch=[pltpu.VMEM((2, LMAX * 8, 128), F32)],
        name="legendre_table",
    )(
        jnp.broadcast_to(order_f, (8, 256)),
        log_start,
        jnp.cos(colat)[None, :],
        (sine * (math.pi / NLAT))[None, :],
    )


def phase_of(rows, cols):
    return 2.0 * math.pi / NLON * (rows * cols % NLON).astype(F32)


def forward_matrix():
    row = jnp.arange(512, dtype=jnp.int32)[:, None]
    order = row // 16 * 8 + row % 8
    imag = row // 8 % 2 == 1
    phase = phase_of(order, jnp.arange(NLON, dtype=jnp.int32)[None, :])
    return jnp.where(imag, -jnp.sin(phase), jnp.cos(phase)) / NLON


def inverse_matrix():
    row = jnp.arange(NLON, dtype=jnp.int32)[:, None]
    inner = row % 96
    lon = inner // 24 * 192 + row // 192 * 48 + inner // 12 % 2 * 24 + row // 96 % 2 * 12 + row % 12
    col = jnp.arange(512, dtype=jnp.int32)[None, :]
    order = col // 16 * 8 + col % 8
    imag = col // 8 % 2 == 1
    phase = phase_of(order, lon)
    return jnp.where(imag, -jnp.sin(phase), jnp.cos(phase)) * jnp.where(order == 0, 1.0, 2.0)


def spread_kernel(south_ref, atm_ref, out_ref):
    south = south_ref[0]
    for yk in range(8):
        for group in range(3):
            tiles = []
            for i in range(4):
                row = 4 * group + i
                tiles.append(atm_ref[yk * 12 + jnp.where(south == 1, 11 - row, row)])
            for z in range(4):
                out_ref[yk // 2 * 8 + z * 2 + yk % 2, :, 128 * group : 128 * group + 128] = pack(
                    [(tile, z) for tile in tiles]
                )


def forward_kernel(in_ref, fh_ref, fl_ref, out_ref, mix_ref):
    for s in range(16):
        north = in_ref[16 * s : 16 * s + 16, :]
        south = in_ref[16 * (31 - s) : 16 * (31 - s) + 16, :]
        for group in range(3):
            lanes = slice(128 * group, 128 * group + 128)
            mix_ref[group, 16 * s : 16 * s + 16, :] = north[:, lanes] + south[:, lanes]
            mix_ref[group, 256 + 16 * s : 256 + 16 * s + 16, :] = north[:, lanes] - south[:, lanes]
    for half in range(2):
        results = []
        for m4 in range(4):
            m = half * 4 + m4
            blocks = []
            for group in range(3):
                parts = [
                    mix_ref[group, pl.ds(base + r * 8 + m, 16, stride=16), :]
                    for base in (0, 256)
                    for r in (0, 1)
                ]
                for i in range(4):
                    blocks.append(pack([(part, i) for part in parts]))
            column = split(jnp.concatenate(blocks, axis=0))
            results.append(
                [dot3((fh_ref[m, parity], fl_ref[m, parity]), column) for parity in range(2)]
            )
        for parity in range(2):
            for r in range(2):
                tile = pack(
                    [(results[m4][parity], 2 * ((m4 + parity) % 2) + r) for m4 in range(4)]
                )
                for z in range(4):
                    out_ref[
                        z * 2 + half, parity * 48 : parity * 48 + 48, 128 * r : 128 * r + 128
                    ] = tile[z * 48 : z * 48 + 48]


def join_kernel(in_ref, out_ref, rows_ref):
    for parity in range(2):
        for t in range(3):
            rows = slice(parity * 48 + t * 16, parity * 48 + t * 16 + 16)
            off = 2 * t + parity
            for mr in range(8):
                lanes = slice(128 * (mr // 4), 128 * (mr // 4) + 128)
                for f in range(2):
                    rows_ref[f, pl.ds(off * 8 + mr, 16, stride=48), :] = pack(
                        [(in_ref[z * 2 + f, rows, lanes], mr % 4) for z in range(4)]
                    )
    for f in range(2):
        out_ref[:, 128 * f : 128 * f + 128] = rows_ref[f]


def part_kernel(in_ref, out_ref, rows_ref):
    for f in range(2):
        rows_ref[f] = in_ref[:, 128 * f : 128 * f + 128]
    for parity in range(2):
        for t in range(3):
            rows = slice(parity * 48 + t * 16, parity * 48 + t * 16 + 16)
            off = 2 * t + parity
            for f in range(2):
                tiles = [
                    rows_ref[f, pl.ds(off * 8 + mr, 16, stride=48), :]
                    for mr in range(8)
                ]
                for z in range(4):
                    for r in range(2):
                        out_ref[z * 2 + f, rows, 128 * r : 128 * r + 128] = pack(
                            [(tiles[4 * r + m4], z) for m4 in range(4)]
                        )


def mix_kernel(in_ref, weight_ref, out_ref):
    for i in range(3):
        value = in_ref[:, i]
        turned = jnp.concatenate([-value[:, 4:], value[:, :4]], axis=1)
        result = dot3(split(value.reshape(256, C)), split(weight_ref[0, i])) + dot3(
            split(turned.reshape(256, C)), split(weight_ref[1, i])
        )
        out_ref[:, i] = result.reshape(32, 8, C)


def inverse_kernel(in_ref, ih_ref, il_ref, out_ref, north_ref, south_ref):
    for half in range(2):
        halves = []
        for parity in range(2):
            halves.append(
                split(
                    jnp.concatenate(
                        [
                            in_ref[z * 2 + half, parity * 48 : parity * 48 + 48, :]
                            for z in range(4)
                        ],
                        axis=0,
                    )
                )
            )
        for m4 in range(4):
            m = half * 4 + m4
            even, odd = (
                dot3((ih_ref[m, parity], il_ref[m, parity]), halves[parity])
                for parity in (m4 % 2, 1 - m4 % 2)
            )
            for r in range(2):
                lanes = slice(128 * r, 128 * r + 128)
                a, b = even[:, lanes], odd[:, lanes]
                for value, ref in ((a + b, north_ref), (a - b, south_ref)):
                    for group in range(3):
                        ref[group, pl.ds(r * 8 + m, 16, stride=16), :] = pack(
                            [
                                (value[(4 * group + i) * 16 : (4 * group + i) * 16 + 16], m4)
                                for i in range(4)
                            ]
                        )
    for group in range(3):
        lanes = slice(128 * group, 128 * group + 128)
        out_ref[:256, lanes] = north_ref[group]
        for s in range(16):
            out_ref[16 * (31 - s) : 16 * (31 - s) + 16, lanes] = south_ref[
                group, 16 * s : 16 * s + 16, :
            ]


def points_kernel(in_ref, out_ref):
    for row in range(12):
        lanes = slice(128 * (row // 4), 128 * (row // 4) + 128)
        for f in range(2):
            tile = pack([(in_ref[z * 2 + f, :, lanes], row % 4) for z in range(4)])
            for yk in range(8):
                out_ref[
                    yk * 144 + row * 12 : yk * 144 + row * 12 + 12, 128 * f : 128 * f + 128
                ] = tile[yk * 12 : yk * 12 + 12]


def finish_kernel(south_ref, in_ref, out_ref):
    south = south_ref[0]
    for yk in range(8):
        for row in range(12):
            place = yk * 12 + jnp.where(south == 1, 11 - row, row)
            out_ref[place] = jnp.concatenate(
                [in_ref[f * 8 + yk, row * 12 : row * 12 + 12, :] for f in range(2)], axis=0
            )


def exchange(blocks, axes):
    return lax.all_to_all(blocks, axes, split_axis=0, concat_axis=0, tiled=True)


def with_halo(block, sides, width):
    for axis, dim in sides:
        count = lax.axis_size(axis)
        forward = [(i, i + 1) for i in range(count - 1)]
        backward = [(target, source) for source, target in forward]
        low = lax.ppermute(
            lax.slice_in_dim(block, block.shape[dim] - width, None, axis=dim), axis, forward
        )
        high_side = lax.ppermute(lax.slice_in_dim(block, 0, width, axis=dim), axis, backward)
        block = jnp.concatenate([low, block, high_side], axis=dim)
    return block


def both(value, axis):
    other = lax.ppermute(value, "feat", [(0, 1), (1, 0)])
    first = lax.axis_index("feat") == 0
    return jnp.concatenate(
        [jnp.where(first, value, other), jnp.where(first, other, value)], axis=axis
    )


def channel_join(matrix):
    return both(matrix, 1)


def gelu(value):
    return jax.nn.gelu(value, approximate=False)


def dense(left, right):
    return jnp.dot(left, right, precision=high, preferred_element_type=F32)


def atmosphere_step(atmosphere, spectral_weight, mlp_in, mlp_out):
    whole_weight = both(spectral_weight, 3)
    whole_in = channel_join(mlp_in)
    whole_out = channel_join(mlp_out)
    south = (lax.axis_index("lat") >= 2).astype(jnp.int32).reshape(1)
    orders = lax.axis_index(ORDER_AXES) * 8 + jnp.arange(8, dtype=jnp.int32)

    spread = local_call(spread_kernel, shape(32, 24, 384), name="spread", smem=1)(south, atmosphere)
    grid = exchange(spread, LON).reshape(NLON, 384)
    tables = legendre_tables(orders)
    spectrum = dense(forward_matrix(), grid)
    spectrum = exchange(spectrum.reshape(32, 16, 384), ORDER_AXES).reshape(512, 384)
    coeffs = local_call(
        forward_kernel, shape(8, 96, 256), [pltpu.VMEM((3, 512, 128), F32)], name="forward"
    )(spectrum, tables[0], tables[1])
    coeffs = exchange(coeffs, CHAN_AXES)
    coeffs = local_call(
        join_kernel, shape(768, 256), [pltpu.VMEM((2, 768, 128), F32)], name="join"
    )(coeffs)
    coeffs = exchange(coeffs.reshape(32, 24, 256), ORDER_AXES).reshape(32, 3, 8, 256)
    mixed = local_call(mix_kernel, shape(32, 3, 8, 256), name="mix")(coeffs, whole_weight)
    mixed = exchange(mixed.reshape(32, 24, 256), ORDER_AXES).reshape(768, 256)
    mixed = local_call(
        part_kernel, shape(8, 96, 256), [pltpu.VMEM((2, 768, 128), F32)], name="part"
    )(mixed)
    mixed = exchange(mixed, CHAN_AXES)
    waves = local_call(
        inverse_kernel, shape(512, 384), [pltpu.VMEM((3, 256, 128), F32)] * 2, name="inverse"
    )(mixed, tables[2], tables[3])
    waves = exchange(waves.reshape(32, 16, 384), ORDER_AXES).reshape(512, 384)
    carried = jnp.transpose(grid.reshape(4, 4, 2, 2, 12, 384), (1, 3, 0, 2, 4, 5))
    summed = carried.reshape(NLON, 384) + dense(inverse_matrix(), waves)
    summed = exchange(summed.reshape(8, 96, 384), CHAN_AXES)
    points = local_call(points_kernel, shape(1152, 256), name="points")(summed)
    hidden = gelu(dense(points, whole_in))
    halves = [
        points[:, 128 * f : 128 * f + 128] + dense(hidden, whole_out[:, 128 * f : 128 * f + 128])
        for f in range(2)
    ]
    result = jnp.stack(halves).reshape(16, 144, 128)
    result = exchange(result, ("feat", "y", "core"))
    return local_call(finish_kernel, shape(96, 24, 128), name="finish", smem=1)(south, result)


def ocean_step(
    atmosphere,
    ocean_state,
    depth_kernel,
    depth_bias,
    norm_gain,
    ocean_up,
    ocean_down,
    ocean_bias,
    layer_scale,
    flux_weight,
    regrid_rows,
    ocean_rows,
    land_mask,
):
    half_chan = atmosphere.shape[2]
    tile_rows, tile_cols, ocean_half = ocean_state.shape
    whole_up = channel_join(ocean_up)
    padded = with_halo(ocean_state, (("lat", 0), (LON, 1)), KERNEL // 2)
    flat_atm = atmosphere.reshape(-1, half_chan)
    picked = jnp.take(flat_atm, regrid_rows.reshape(-1), axis=0).reshape(32, -1, half_chan)
    arrived = exchange(picked, LON)
    conv = jnp.zeros((tile_rows, tile_cols, ocean_half), F32) + depth_bias
    for tap_row in range(KERNEL):
        for tap_col in range(KERNEL):
            conv = (
                conv
                + padded[tap_row : tap_row + tile_rows, tap_col : tap_col + tile_cols]
                * depth_kernel[tap_row, tap_col]
            )
    arrived_full = channel_join(arrived.reshape(-1, half_chan))
    flux_rows = dense(arrived_full, flux_weight)
    forcing = jnp.take(flux_rows, ocean_rows.reshape(-1), axis=0).reshape(
        tile_rows, tile_cols, ocean_half
    )
    joined = conv + forcing
    full_rows = channel_join(joined.reshape(-1, ocean_half))
    row_mean = jnp.mean(full_rows, axis=-1, keepdims=True)
    centered = full_rows - row_mean
    variance = jnp.mean(centered * centered, axis=-1, keepdims=True)
    normed = centered * lax.rsqrt(variance + 1e-06) * norm_gain
    update = dense(gelu(dense(normed, whole_up)), ocean_down) + ocean_bias
    mask_rows = tile_rows // BLOCK
    mask_cols = tile_cols // BLOCK
    cell_mask = (
        jnp.broadcast_to(land_mask[:, None, :, None], (mask_rows, BLOCK, mask_cols, BLOCK))
        .reshape(tile_rows, tile_cols)
        .astype(F32)
    )
    return ocean_state + cell_mask[:, :, None] * layer_scale * update.reshape(
        tile_rows, tile_cols, ocean_half
    )


def shards(
    atmosphere,
    spectral_weight,
    mlp_in,
    mlp_out,
    ocean_state,
    depth_kernel,
    depth_bias,
    norm_gain,
    ocean_up,
    ocean_down,
    ocean_bias,
    layer_scale,
    flux_weight,
    regrid_rows,
    ocean_rows,
    land_mask,
):
    atmos_next = atmosphere_step(atmosphere, spectral_weight, mlp_in, mlp_out)
    ocean_next = ocean_step(
        atmosphere,
        ocean_state,
        depth_kernel,
        depth_bias,
        norm_gain,
        ocean_up,
        ocean_down,
        ocean_bias,
        layer_scale,
        flux_weight,
        regrid_rows,
        ocean_rows,
        land_mask,
    )
    return atmos_next, ocean_next


def solution(mesh):
    fine = Mesh(mesh.devices.reshape(4, 4, 4, 2, 2), ("lat", "y", "zh", "core", "feat"))
    in_specs = (
        P("lat", LON, "feat"),
        P(None, ("lat",) + LON, None, "feat"),
        P(None, "feat"),
        P(None, "feat"),
        P("lat", LON, "feat"),
        P(None, None, "feat"),
        P("feat"),
        P(),
        P(None, "feat"),
        P(None, "feat"),
        P("feat"),
        P("feat"),
        P(None, "feat"),
        P("lat", LON, None, None),
        P("lat", LON),
        P("lat", LON),
    )
    out_specs = (P("lat", LON, "feat"), P("lat", LON, "feat"))
    return jax.shard_map(shards, mesh=fine, in_specs=in_specs, out_specs=out_specs, check_vma=False)
```

```python
import functools
import math

import jax
import jax.numpy as jnp
from jax import lax
from jax.experimental import pallas as pl
from jax.experimental.pallas import tpu as pltpu
from jax.sharding import Mesh, PartitionSpec as P

C = 256
NLAT = 384
NLON = 768
LMAX = 384
MMAX = 256
KERNEL = 7
BLOCK = 8

LON = ("y", "zh", "core")
ORDER_AXES = ("lat", "y", "core")
CHAN_AXES = ("zh", "feat")
F32 = jnp.float32
BF16 = jnp.bfloat16
high = lax.Precision.HIGH


def split(value):
    upper = value.astype(BF16)
    return upper, (value - upper.astype(F32)).astype(BF16)


def mm(left, right):
    return jnp.dot(left, right, preferred_element_type=F32)


def dot3(left, right):
    return mm(left[0], right[0]) + (mm(left[0], right[1]) + mm(left[1], right[0]))


def pack(pieces):
    place = lax.broadcasted_iota(jnp.int32, pieces[0][0].shape, 1) // 32
    out = None
    for i, (tile, chunk) in enumerate(pieces):
        shift = (32 * (i - chunk)) % 128
        moved = tile if shift == 0 else pltpu.roll(tile, shift, 1)
        out = moved if out is None else jnp.where(place == i, moved, out)
    return out


def local_call(kernel, out_shape, scratch=(), name=None, smem=0):
    def run(*args):
        specs = [pl.BlockSpec(memory_space=pltpu.SMEM)] * smem
        specs += [pl.BlockSpec(memory_space=pltpu.VMEM)] * (len(args) - smem)
        return pl.pallas_call(
            kernel,
            out_shape=out_shape,
            in_specs=specs,
            out_specs=jax.tree.map(lambda _: pl.BlockSpec(memory_space=pltpu.VMEM), out_shape),
            scratch_shapes=list(scratch),
            name=name,
        )(*args)

    return run


def shape(*dims, dtype=F32):
    return jax.ShapeDtypeStruct(dims, dtype)


def table_kernel(order_ref, start_ref, cos_ref, quad_ref, fh_ref, fl_ref, ih_ref, il_ref, rows_ref):
    order = order_ref[...]
    order_sq = order * order
    cosine = jnp.broadcast_to(cos_ref[...], order.shape)
    start = start_ref[...]

    def six(group, carry):
        current, previous, shift = carry
        for off in range(6):
            deg = jnp.full(order.shape, group * 6 + off, jnp.int32).astype(F32)
            factor_a = jnp.sqrt(
                jnp.maximum(4.0 * deg * deg - 1.0, 0.0) / jnp.maximum(deg * deg - order_sq, 1.0)
            )
            below = deg - 1.0
            factor_b = jnp.sqrt(
                jnp.maximum(below * below - order_sq, 0.0)
                / jnp.maximum(4.0 * below * below - 1.0, 1.0)
            )
            recurred = factor_a * (cosine * current - factor_b * previous)
            fresh = jnp.where(deg == order, 1.0, jnp.where(deg > order, recurred, 0.0))
            large = jnp.abs(fresh) > 2.0**32
            rescale = jnp.where(large, 2.0 ** (-32), 1.0)
            fresh = fresh * rescale
            shift = shift + jnp.where(large, 32.0, 0.0)
            value = fresh * jnp.exp(start + shift * math.log(2.0))
            pos = (off % 2) * 192 + (group % 4) * 48 + (off // 2) * 16 + group // 4
            where = pl.ds(pl.multiple_of(pos * 8, 8), 8)
            rows_ref[0, where, :] = value[:, :128]
            rows_ref[1, where, :] = value[:, 128:]
            previous = current * rescale
            current = fresh
        return current, previous, shift

    zeros = jnp.zeros(order.shape, F32)
    lax.fori_loop(0, LMAX // 6, six, (zeros, zeros, zeros))
    quad = quad_ref[...]
    for m in range(8):
        for parity in range(2):
            part = jnp.concatenate(
                [rows_ref[g, pl.ds(parity * 1536 + m, 192, stride=8), :] for g in range(2)], axis=1
            )
            upper, lower = split(part * quad)
            fh_ref[m, parity] = upper[:, :192]
            fl_ref[m, parity] = lower[:, :192]
            turned = jnp.transpose(part)[:192]
            upper, lower = split(turned)
            ih_ref[m, parity] = upper
            il_ref[m, parity] = lower


def legendre_tables(orders):
    column = jnp.arange(256, dtype=jnp.int32)
    lat_id = jnp.where(column < 192, 12 * (column % 16) + column // 16, 0).astype(F32)
    colat = math.pi * (lat_id + 0.5) / NLAT
    sine = jnp.sin(colat)
    order_f = orders.astype(F32)[:, None]
    steps_k = jnp.arange(1, MMAX + 1, dtype=jnp.int32)
    step_f = steps_k.astype(F32)
    log_terms = jnp.log((2.0 * step_f + 1.0) / (2.0 * step_f))
    log_norm = jnp.sum(
        jnp.where(steps_k[None, :] <= orders[:, None], log_terms[None, :], 0.0), axis=1
    )
    log_start = 0.5 * (math.log(0.5) + log_norm[:, None]) + order_f * jnp.log(sine)[None, :]
    return local_call(
        table_kernel,
        (
            shape(8, 2, 192, 192, dtype=BF16),
            shape(8, 2, 192, 192, dtype=BF16),
            shape(8, 2, 192, 192, dtype=BF16),
            shape(8, 2, 192, 192, dtype=BF16),
        ),
        scratch=[pltpu.VMEM((2, LMAX * 8, 128), F32)],
        name="legendre_table",
    )(
        jnp.broadcast_to(order_f, (8, 256)),
        log_start,
        jnp.cos(colat)[None, :],
        (sine * (math.pi / NLAT))[None, :],
    )


def cosine_parts(order, lon, imag):
    turn = (order * lon + jnp.where(imag, NLON // 4, 0)) % NLON
    return jnp.cos(2.0 * math.pi / NLON * turn.astype(F32))


def parts_of(value):
    upper = lax.reduce_precision(value, 8, 7)
    return upper.astype(BF16), (value - upper).astype(BF16)


def forward_matrix(zero):
    row = jnp.arange(512, dtype=jnp.int32)[:, None] + zero
    order = row % 256 // 8 * 8 + row % 4 * 2 + row // 256
    lon = jnp.arange(NLON // 2, dtype=jnp.int32)[None, :]
    return parts_of(cosine_parts(order, lon, row // 4 % 2 == 1) / NLON)


def inverse_matrix(zero):
    lon = jnp.arange(NLON // 2, dtype=jnp.int32)[:, None] + zero
    col = jnp.arange(512, dtype=jnp.int32)[None, :]
    order = col % 256 // 8 * 8 + col % 4 * 2 + col // 256
    return parts_of(
        cosine_parts(order, lon, col // 4 % 2 == 1) * jnp.where(order == 0, 1.0, 2.0)
    )


def spread_kernel(south_ref, atm_ref, out_ref):
    south = south_ref[0]
    for yk in range(8):
        for group in range(3):
            tiles = []
            for i in range(4):
                row = 4 * group + i
                tiles.append(atm_ref[yk * 12 + jnp.where(south == 1, 11 - row, row)])
            for z in range(4):
                out_ref[yk // 2 * 8 + z * 2 + yk % 2, :, 128 * group : 128 * group + 128] = pack(
                    [(tile, z) for tile in tiles]
                )


def fourier_kernel(upper_ref, lower_ref, in_ref, out_ref):
    near, far = in_ref[: NLON // 2, :], in_ref[NLON // 2 :, :]
    even = dot3((upper_ref[:256, :], lower_ref[:256, :]), split(near + far)).reshape(32, 8, 384)
    odd = dot3((upper_ref[256:, :], lower_ref[256:, :]), split(near - far)).reshape(32, 8, 384)
    out_ref[:, 0] = jnp.concatenate([even[:, :4], odd[:, :4]], axis=1)
    out_ref[:, 1] = jnp.concatenate([even[:, 4:], odd[:, 4:]], axis=1)


def synthesis_kernel(upper_ref, lower_ref, in_ref, grid_ref, out_ref):
    real, imag = in_ref[:, 0], in_ref[:, 1]
    even = split(jnp.concatenate([real[:, :4], imag[:, :4]], axis=1).reshape(256, 384))
    odd = split(jnp.concatenate([real[:, 4:], imag[:, 4:]], axis=1).reshape(256, 384))
    for y in range(2):
        block = slice(192 * y, 192 * y + 192)
        parts = [
            dot3((upper_ref[block, lanes], lower_ref[block, lanes]), waves)
            for lanes, waves in ((slice(0, 256), even), (slice(256, 512), odd))
        ]
        for far in range(2):
            wave = parts[0] - parts[1] if far else parts[0] + parts[1]
            first = 192 * y + 384 * far
            value = grid_ref[first : first + 192, :] + wave
            for z in range(4):
                for k in range(2):
                    for f in range(2):
                        source = 48 * z + 24 * k + 12 * f
                        place = 12 * (2 * (y + 2 * far) + k)
                        out_ref[z * 2 + f, place : place + 12, :] = value[source : source + 12]


def forward_kernel(in_ref, fh_ref, fl_ref, out_ref, mix_ref):
    for s in range(16):
        north = in_ref[16 * s : 16 * s + 16, :]
        south = in_ref[16 * (31 - s) : 16 * (31 - s) + 16, :]
        for group in range(3):
            lanes = slice(128 * group, 128 * group + 128)
            mix_ref[group, 16 * s : 16 * s + 16, :] = north[:, lanes] + south[:, lanes]
            mix_ref[group, 256 + 16 * s : 256 + 16 * s + 16, :] = north[:, lanes] - south[:, lanes]
    for half in range(2):
        results = []
        for m4 in range(4):
            m = half * 4 + m4
            blocks = []
            for group in range(3):
                parts = [
                    mix_ref[group, pl.ds(base + r * 8 + m, 16, stride=16), :]
                    for base in (0, 256)
                    for r in (0, 1)
                ]
                for i in range(4):
                    blocks.append(pack([(part, i) for part in parts]))
            column = split(jnp.concatenate(blocks, axis=0))
            results.append(
                [dot3((fh_ref[m, parity], fl_ref[m, parity]), column) for parity in range(2)]
            )
        for parity in range(2):
            for r in range(2):
                tile = pack(
                    [(results[m4][parity], 2 * ((half + parity) % 2) + r) for m4 in range(4)]
                )
                for z in range(4):
                    out_ref[
                        z * 2 + half, parity * 48 : parity * 48 + 48, 128 * r : 128 * r + 128
                    ] = tile[z * 48 : z * 48 + 48]


def join_kernel(in_ref, out_ref, rows_ref):
    for parity in range(2):
        for t in range(3):
            rows = slice(parity * 48 + t * 16, parity * 48 + t * 16 + 16)
            off = 2 * t + parity
            for mr in range(8):
                lanes = slice(128 * (mr // 4), 128 * (mr // 4) + 128)
                for f in range(2):
                    rows_ref[f, pl.ds(off * 8 + mr, 16, stride=48), :] = pack(
                        [(in_ref[z * 2 + f, rows, lanes], mr % 4) for z in range(4)]
                    )
    for f in range(2):
        out_ref[:, 128 * f : 128 * f + 128] = rows_ref[f]


def part_kernel(in_ref, out_ref, rows_ref):
    for f in range(2):
        rows_ref[f] = in_ref[:, 128 * f : 128 * f + 128]
    for parity in range(2):
        for t in range(3):
            rows = slice(parity * 48 + t * 16, parity * 48 + t * 16 + 16)
            off = 2 * t + parity
            for f in range(2):
                tiles = [
                    rows_ref[f, pl.ds(off * 8 + mr, 16, stride=48), :]
                    for mr in range(8)
                ]
                for z in range(4):
                    for r in range(2):
                        out_ref[z * 2 + f, rows, 128 * r : 128 * r + 128] = pack(
                            [(tiles[4 * r + m4], z) for m4 in range(4)]
                        )


def mix_kernel(feat_ref, in_ref, own_ref, other_ref, out_ref):
    first = feat_ref[0] == 0
    for i in range(3):
        weights = []
        for r in range(2):
            own, other = own_ref[r, i], other_ref[r, i]
            weights.append(
                split(
                    jnp.concatenate(
                        [jnp.where(first, own, other), jnp.where(first, other, own)], axis=1
                    )
                )
            )
        value = in_ref[:, i]
        turned = jnp.concatenate([-value[:, 4:], value[:, :4]], axis=1)
        result = dot3(split(value.reshape(256, C)), weights[0]) + dot3(
            split(turned.reshape(256, C)), weights[1]
        )
        out_ref[:, i] = result.reshape(32, 8, C)


def inverse_kernel(in_ref, ih_ref, il_ref, out_ref, north_ref, south_ref):
    for half in range(2):
        halves = []
        for parity in range(2):
            halves.append(
                split(
                    jnp.concatenate(
                        [
                            in_ref[z * 2 + half, parity * 48 : parity * 48 + 48, :]
                            for z in range(4)
                        ],
                        axis=0,
                    )
                )
            )
        for m4 in range(4):
            m = half * 4 + m4
            even, odd = (
                dot3((ih_ref[m, parity], il_ref[m, parity]), halves[parity])
                for parity in (half, 1 - half)
            )
            for r in range(2):
                lanes = slice(128 * r, 128 * r + 128)
                a, b = even[:, lanes], odd[:, lanes]
                for value, ref in ((a + b, north_ref), (a - b, south_ref)):
                    for group in range(3):
                        ref[group, pl.ds(r * 8 + m, 16, stride=16), :] = pack(
                            [
                                (value[(4 * group + i) * 16 : (4 * group + i) * 16 + 16], m4)
                                for i in range(4)
                            ]
                        )
    for group in range(3):
        lanes = slice(128 * group, 128 * group + 128)
        out_ref[:256, lanes] = north_ref[group]
        for s in range(16):
            out_ref[16 * (31 - s) : 16 * (31 - s) + 16, lanes] = south_ref[
                group, 16 * s : 16 * s + 16, :
            ]


def points_kernel(in_ref, out_ref):
    for row in range(12):
        lanes = slice(128 * (row // 4), 128 * (row // 4) + 128)
        for f in range(2):
            tile = pack([(in_ref[z * 2 + f, :, lanes], row % 4) for z in range(4)])
            for yk in range(8):
                out_ref[
                    yk * 144 + row * 12 : yk * 144 + row * 12 + 12, 128 * f : 128 * f + 128
                ] = tile[yk * 12 : yk * 12 + 12]


def finish_kernel(south_ref, in_ref, out_ref):
    south = south_ref[0]
    for yk in range(8):
        for row in range(12):
            place = yk * 12 + jnp.where(south == 1, 11 - row, row)
            out_ref[place] = jnp.concatenate(
                [in_ref[f * 8 + yk, row * 12 : row * 12 + 12, :] for f in range(2)], axis=0
            )


def exchange(blocks, axes):
    return lax.all_to_all(blocks, axes, split_axis=0, concat_axis=0, tiled=True)


def with_halo(block, sides, width):
    for axis, dim in sides:
        count = lax.axis_size(axis)
        forward = [(i, i + 1) for i in range(count - 1)]
        backward = [(target, source) for source, target in forward]
        low = lax.ppermute(
            lax.slice_in_dim(block, block.shape[dim] - width, None, axis=dim), axis, forward
        )
        high_side = lax.ppermute(lax.slice_in_dim(block, 0, width, axis=dim), axis, backward)
        block = jnp.concatenate([low, block, high_side], axis=dim)
    return block


def partner(value):
    return lax.ppermute(value, "feat", [(0, 1), (1, 0)])


def together(*values):
    return lax.optimization_barrier(values)


def shift_out(blocks, axis):
    count = lax.axis_size(axis)
    me = lax.axis_index(axis)
    got = [lax.dynamic_index_in_dim(blocks, me, 0, keepdims=False)]
    for d in range(1, count):
        sent = lax.dynamic_index_in_dim(blocks, (me + d) % count, 0, keepdims=False)
        got.append(lax.ppermute(sent, axis, [(i, (i + d) % count) for i in range(count)]))
    return tuple(got)


def shift_in(got, axis):
    count = lax.axis_size(axis)
    me = lax.axis_index(axis)
    stacked = jnp.stack(got)
    return jnp.stack(
        [lax.dynamic_index_in_dim(stacked, (me - i) % count, 0, keepdims=False) for i in range(count)]
    )


def plane_piece(matrices):
    place = lax.axis_index(("y", "core"))
    pieces = []
    for matrix in matrices:
        rows = matrix.shape[0] // 8
        part = lax.dynamic_slice_in_dim(matrix, place * rows, rows, 0)
        pieces += [part[:, c : c + 128] for c in range(0, matrix.shape[1], 128)]
    return jnp.concatenate(pieces, axis=0)


def plane_pair(piece):
    return both(piece, lax.ppermute(piece, "core", [(0, 1), (1, 0)]), 0, "core")


def plane_gather(pair):
    return (pair,) + tuple(
        lax.ppermute(pair, "y", [(i, (i + d) % 4) for i in range(4)]) for d in range(1, 4)
    )


def plane_join(got, matrices):
    whole = shift_in(got, "y").reshape(8, -1, 128)
    joined = []
    first = 0
    for matrix in matrices:
        rows, wide = matrix.shape[0] // 8, matrix.shape[1] // 128
        part = whole[:, first : first + rows * wide].reshape(8, wide, rows, 128)
        joined.append(jnp.transpose(part, (0, 2, 1, 3)).reshape(matrix.shape))
        first += rows * wide
    return joined


def both(value, other, axis, mesh_axis="feat"):
    first = lax.axis_index(mesh_axis) == 0
    return jnp.concatenate(
        [jnp.where(first, value, other), jnp.where(first, other, value)], axis=axis
    )


def gelu(value):
    return 0.5 * value * (1.0 + lax.erf(value * math.sqrt(0.5)))


def dense(left, right):
    return jnp.dot(left, right, precision=high, preferred_element_type=F32)


def convolve(padded, depth_kernel, depth_bias, tile_rows, tile_cols):
    conv = jnp.zeros((tile_rows, tile_cols, padded.shape[2]), F32) + depth_bias
    for tap_row in range(KERNEL):
        for tap_col in range(KERNEL):
            conv = (
                conv
                + padded[tap_row : tap_row + tile_rows, tap_col : tap_col + tile_cols]
                * depth_kernel[tap_row, tap_col]
            )
    return conv


def shards(
    atmosphere,
    spectral_weight,
    mlp_in,
    mlp_out,
    ocean_state,
    depth_kernel,
    depth_bias,
    norm_gain,
    ocean_up,
    ocean_down,
    ocean_bias,
    layer_scale,
    flux_weight,
    regrid_rows,
    ocean_rows,
    land_mask,
):
    half_chan = atmosphere.shape[2]
    tile_rows, tile_cols, ocean_half = ocean_state.shape
    south = (lax.axis_index("lat") >= 2).astype(jnp.int32).reshape(1)
    feat = lax.axis_index("feat").reshape(1)
    eight = jnp.arange(8, dtype=jnp.int32)
    orders = lax.axis_index(ORDER_AXES) * 8 + eight % 4 * 2 + eight // 4
    zero = jnp.int32(0) * feat[0]

    spread = local_call(spread_kernel, shape(32, 24, 384), name="spread", smem=1)(south, atmosphere)
    spread, flat_atm, state, orders, early = together(
        spread, atmosphere.reshape(-1, half_chan), ocean_state, orders, zero
    )
    grid = exchange(spread, LON).reshape(NLON, 384)
    forward_parts = forward_matrix(early)
    tables = legendre_tables(orders)
    picked = flat_atm.at[regrid_rows.reshape(-1)].get(mode="promise_in_bounds")
    picked = jnp.moveaxis(picked.reshape(4, 4, 2, -1, half_chan), 2, 0)
    picked = shift_out(picked, "core")
    tall = with_halo(state, (("lat", 0),), KERNEL // 2)
    grid, forward_parts, tables = together(grid, forward_parts, tables)
    spectrum = local_call(fourier_kernel, shape(32, 2, 8, 384), name="fourier")(
        *forward_parts, grid
    )

    spectrum, weight, tall, picked, shared = together(
        spectrum, spectral_weight, tall, picked, (mlp_in, mlp_out, ocean_up)
    )
    spectrum = exchange(spectrum.reshape(32, 16, 384), ORDER_AXES).reshape(512, 384)
    other_weight = partner(weight)
    piece = partner(plane_piece(shared))
    picked = jnp.moveaxis(shift_in(picked, "core"), 0, 2)
    coeffs = local_call(
        forward_kernel, shape(8, 96, 256), [pltpu.VMEM((3, 512, 128), F32)], name="forward"
    )(spectrum, tables[0], tables[1])

    coeffs, other_weight, picked = together(coeffs, other_weight, picked)
    coeffs = exchange(coeffs, CHAN_AXES)
    picked = shift_out(picked, "y")
    coeffs, picked, piece = together(coeffs, picked, piece)
    coeffs = local_call(
        join_kernel, shape(768, 256), [pltpu.VMEM((2, 768, 128), F32)], name="join"
    )(coeffs)

    coeffs, picked = together(coeffs, shift_in(picked, "y"))
    coeffs = exchange(coeffs.reshape(32, 24, 256), ORDER_AXES).reshape(32, 3, 8, 256)
    arrived = shift_out(jnp.moveaxis(picked, 1, 0), "zh")
    mixed = local_call(mix_kernel, shape(32, 3, 8, 256), name="mix", smem=1)(
        feat, coeffs, weight, other_weight
    )

    mixed, arrived, tall, piece = together(mixed, arrived, tall, piece)
    mixed = exchange(mixed.reshape(32, 24, 256), ORDER_AXES).reshape(768, 256)
    arrived = jnp.moveaxis(shift_in(arrived, "zh"), 0, 1).reshape(-1, half_chan)
    other_arrived = partner(arrived)
    padded = with_halo(tall, ((LON, 1),), KERNEL // 2)
    pair = plane_pair(piece)
    mixed = local_call(
        part_kernel, shape(8, 96, 256), [pltpu.VMEM((2, 768, 128), F32)], name="part"
    )(mixed)

    mixed, other_arrived, pair, late = together(mixed, other_arrived, pair, zero)
    mixed = exchange(mixed, CHAN_AXES)
    inverse_parts = inverse_matrix(late)
    flux_rows = dense(both(arrived, other_arrived, 1), flux_weight)
    forcing = flux_rows.at[ocean_rows.reshape(-1)].get(mode="promise_in_bounds")
    conv = convolve(padded, depth_kernel, depth_bias, tile_rows, tile_cols)
    joined = conv.reshape(-1, ocean_half) + forcing
    pieces = plane_gather(pair)
    mixed, joined, inverse_parts = together(mixed, joined, inverse_parts)
    waves = local_call(
        inverse_kernel, shape(512, 384), [pltpu.VMEM((3, 256, 128), F32)] * 2, name="inverse"
    )(mixed, tables[2], tables[3])

    waves, joined, pieces = together(waves, joined, pieces)
    waves = exchange(waves.reshape(32, 16, 384), ORDER_AXES).reshape(32, 2, 8, 384)
    other_joined = partner(joined)
    summed = local_call(synthesis_kernel, shape(8, 96, 384), name="synthesis")(
        *inverse_parts, waves, grid
    )

    summed, other_joined, pieces = together(summed, other_joined, pieces)
    summed = exchange(summed, CHAN_AXES)
    other_in, other_out, other_up = plane_join(pieces, shared)
    whole_up = both(ocean_up, other_up, 1)
    whole_in = both(mlp_in, other_in, 1)
    whole_out = both(mlp_out, other_out, 1)
    full_rows = both(joined, other_joined, 1)
    row_mean = jnp.mean(full_rows, axis=-1, keepdims=True)
    centered = full_rows - row_mean
    variance = jnp.mean(centered * centered, axis=-1, keepdims=True)
    normed = centered * lax.rsqrt(variance + 1e-06) * norm_gain
    update = dense(gelu(dense(normed, whole_up)), ocean_down) + ocean_bias
    mask_rows = tile_rows // BLOCK
    mask_cols = tile_cols // BLOCK
    cell_mask = (
        jnp.broadcast_to(land_mask[:, None, :, None], (mask_rows, BLOCK, mask_cols, BLOCK))
        .reshape(tile_rows, tile_cols)
        .astype(F32)
    )
    ocean_next = ocean_state + cell_mask[:, :, None] * layer_scale * update.reshape(
        tile_rows, tile_cols, ocean_half
    )
    summed, whole_in, whole_out, ocean_next = together(summed, whole_in, whole_out, ocean_next)
    points = local_call(points_kernel, shape(1152, 256), name="points")(summed)
    hidden = gelu(dense(points, whole_in))
    halves = [
        points[:, 128 * f : 128 * f + 128] + dense(hidden, whole_out[:, 128 * f : 128 * f + 128])
        for f in range(2)
    ]
    result = exchange(jnp.stack(halves).reshape(16, 144, 128), ("feat", "y", "core"))
    atmos_next = local_call(finish_kernel, shape(96, 24, 128), name="finish", smem=1)(south, result)
    return atmos_next, ocean_next


def solution(mesh):
    fine = Mesh(mesh.devices.reshape(4, 4, 4, 2, 2), ("lat", "y", "zh", "core", "feat"))
    in_specs = (
        P("lat", LON, "feat"),
        P(None, ("lat",) + LON, None, "feat"),
        P(None, "feat"),
        P(None, "feat"),
        P("lat", LON, "feat"),
        P(None, None, "feat"),
        P("feat"),
        P(),
        P(None, "feat"),
        P(None, "feat"),
        P("feat"),
        P("feat"),
        P(None, "feat"),
        P("lat", LON, None, None),
        P("lat", LON),
        P("lat", LON),
    )
    out_specs = (P("lat", LON, "feat"), P("lat", LON, "feat"))
    return jax.shard_map(shards, mesh=fine, in_specs=in_specs, out_specs=out_specs, check_vma=False)
```

```python
import functools
import math

import jax
import jax.numpy as jnp
from jax import lax
from jax.experimental import pallas as pl
from jax.experimental.pallas import tpu as pltpu
from jax.sharding import Mesh, PartitionSpec as P

C = 256
NLAT = 384
NLON = 768
LMAX = 384
MMAX = 256
KERNEL = 7
BLOCK = 8

LON = ("y", "zh", "core")
ORDER_AXES = ("lat", "y", "core")
CHAN_AXES = ("zh", "feat")
F32 = jnp.float32
BF16 = jnp.bfloat16
high = lax.Precision.HIGH


def split(value):
    upper = value.astype(BF16)
    return upper, (value - upper.astype(F32)).astype(BF16)


def mm(left, right):
    return jnp.dot(left, right, preferred_element_type=F32)


def dot3(left, right):
    return mm(left[0], right[0]) + (mm(left[0], right[1]) + mm(left[1], right[0]))


def pack(pieces):
    place = lax.broadcasted_iota(jnp.int32, pieces[0][0].shape, 1) // 32
    out = None
    for i, (tile, chunk) in enumerate(pieces):
        shift = (32 * (i - chunk)) % 128
        moved = tile if shift == 0 else pltpu.roll(tile, shift, 1)
        out = moved if out is None else jnp.where(place == i, moved, out)
    return out


def local_call(kernel, out_shape, scratch=(), name=None, smem=0):
    def run(*args):
        specs = [pl.BlockSpec(memory_space=pltpu.SMEM)] * smem
        specs += [pl.BlockSpec(memory_space=pltpu.VMEM)] * (len(args) - smem)
        return pl.pallas_call(
            kernel,
            out_shape=out_shape,
            in_specs=specs,
            out_specs=jax.tree.map(lambda _: pl.BlockSpec(memory_space=pltpu.VMEM), out_shape),
            scratch_shapes=list(scratch),
            name=name,
        )(*args)

    return run


def shape(*dims, dtype=F32):
    return jax.ShapeDtypeStruct(dims, dtype)


def table_kernel(order_ref, start_ref, cos_ref, quad_ref, fh_ref, fl_ref, ih_ref, il_ref, rows_ref):
    order = order_ref[...]
    order_sq = order * order
    cosine = jnp.broadcast_to(cos_ref[...], order.shape)
    start = start_ref[...]

    def six(group, carry):
        current, previous, shift = carry
        for off in range(6):
            deg = jnp.full(order.shape, group * 6 + off, jnp.int32).astype(F32)
            factor_a = jnp.sqrt(
                jnp.maximum(4.0 * deg * deg - 1.0, 0.0) / jnp.maximum(deg * deg - order_sq, 1.0)
            )
            below = deg - 1.0
            factor_b = jnp.sqrt(
                jnp.maximum(below * below - order_sq, 0.0)
                / jnp.maximum(4.0 * below * below - 1.0, 1.0)
            )
            recurred = factor_a * (cosine * current - factor_b * previous)
            fresh = jnp.where(deg == order, 1.0, jnp.where(deg > order, recurred, 0.0))
            large = jnp.abs(fresh) > 2.0**32
            rescale = jnp.where(large, 2.0 ** (-32), 1.0)
            fresh = fresh * rescale
            shift = shift + jnp.where(large, 32.0, 0.0)
            value = fresh * jnp.exp(start + shift * math.log(2.0))
            pos = (off % 2) * 192 + (group % 4) * 48 + (off // 2) * 16 + group // 4
            where = pl.ds(pl.multiple_of(pos * 8, 8), 8)
            rows_ref[0, where, :] = value[:, :128]
            rows_ref[1, where, :] = value[:, 128:]
            previous = current * rescale
            current = fresh
        return current, previous, shift

    zeros = jnp.zeros(order.shape, F32)
    lax.fori_loop(0, LMAX // 6, six, (zeros, zeros, zeros))
    quad = quad_ref[...]
    for m in range(8):
        for parity in range(2):
            part = jnp.concatenate(
                [rows_ref[g, pl.ds(parity * 1536 + m, 192, stride=8), :] for g in range(2)], axis=1
            )
            upper, lower = split(part * quad)
            fh_ref[m, parity] = upper[:, :192]
            fl_ref[m, parity] = lower[:, :192]
            turned = jnp.transpose(part)[:192]
            upper, lower = split(turned)
            ih_ref[m, parity] = upper
            il_ref[m, parity] = lower


def legendre_tables(orders):
    column = jnp.arange(256, dtype=jnp.int32)
    lat_id = jnp.where(column < 192, 12 * (column % 16) + column // 16, 0).astype(F32)
    colat = math.pi * (lat_id + 0.5) / NLAT
    sine = jnp.sin(colat)
    order_f = orders.astype(F32)[:, None]
    steps_k = jnp.arange(1, MMAX + 1, dtype=jnp.int32)
    step_f = steps_k.astype(F32)
    log_terms = jnp.log((2.0 * step_f + 1.0) / (2.0 * step_f))
    log_norm = jnp.sum(
        jnp.where(steps_k[None, :] <= orders[:, None], log_terms[None, :], 0.0), axis=1
    )
    log_start = 0.5 * (math.log(0.5) + log_norm[:, None]) + order_f * jnp.log(sine)[None, :]
    return local_call(
        table_kernel,
        (
            shape(8, 2, 192, 192, dtype=BF16),
            shape(8, 2, 192, 192, dtype=BF16),
            shape(8, 2, 192, 192, dtype=BF16),
            shape(8, 2, 192, 192, dtype=BF16),
        ),
        scratch=[pltpu.VMEM((2, LMAX * 8, 128), F32)],
        name="legendre_table",
    )(
        jnp.broadcast_to(order_f, (8, 256)),
        log_start,
        jnp.cos(colat)[None, :],
        (sine * (math.pi / NLAT))[None, :],
    )


def cosine_parts(order, lon, imag):
    turn = (order * lon + jnp.where(imag, NLON // 4, 0)) % NLON
    return jnp.cos(2.0 * math.pi / NLON * turn.astype(F32))


def parts_of(value):
    upper = lax.reduce_precision(value, 8, 7)
    return upper.astype(BF16), (value - upper).astype(BF16)


def forward_matrix(zero):
    row = jnp.arange(512, dtype=jnp.int32)[:, None] + zero
    order = row % 256 // 8 * 8 + row % 4 * 2 + row // 256
    lon = jnp.arange(NLON // 2, dtype=jnp.int32)[None, :]
    return parts_of(cosine_parts(order, lon, row // 4 % 2 == 1) / NLON)


def inverse_matrix(zero):
    lon = jnp.arange(NLON // 2, dtype=jnp.int32)[:, None] + zero
    col = jnp.arange(512, dtype=jnp.int32)[None, :]
    order = col % 256 // 8 * 8 + col % 4 * 2 + col // 256
    return parts_of(
        cosine_parts(order, lon, col // 4 % 2 == 1) * jnp.where(order == 0, 1.0, 2.0)
    )


def spread_kernel(south_ref, atm_ref, out_ref):
    south = south_ref[0]
    for yk in range(8):
        for group in range(3):
            tiles = []
            for i in range(4):
                row = 4 * group + i
                tiles.append(atm_ref[yk * 12 + jnp.where(south == 1, 11 - row, row)])
            for z in range(4):
                out_ref[yk // 2 * 8 + z * 2 + yk % 2, :, 128 * group : 128 * group + 128] = pack(
                    [(tile, z) for tile in tiles]
                )


def fourier_kernel(upper_ref, lower_ref, in_ref, out_ref):
    near, far = in_ref[: NLON // 2, :], in_ref[NLON // 2 :, :]
    even = dot3((upper_ref[:256, :], lower_ref[:256, :]), split(near + far)).reshape(32, 8, 384)
    odd = dot3((upper_ref[256:, :], lower_ref[256:, :]), split(near - far)).reshape(32, 8, 384)
    out_ref[:, 0] = jnp.concatenate([even[:, :4], odd[:, :4]], axis=1)
    out_ref[:, 1] = jnp.concatenate([even[:, 4:], odd[:, 4:]], axis=1)


def synthesis_kernel(upper_ref, lower_ref, in_ref, grid_ref, out_ref):
    real, imag = in_ref[:, 0], in_ref[:, 1]
    even = split(jnp.concatenate([real[:, :4], imag[:, :4]], axis=1).reshape(256, 384))
    odd = split(jnp.concatenate([real[:, 4:], imag[:, 4:]], axis=1).reshape(256, 384))
    for y in range(2):
        block = slice(192 * y, 192 * y + 192)
        parts = [
            dot3((upper_ref[block, lanes], lower_ref[block, lanes]), waves)
            for lanes, waves in ((slice(0, 256), even), (slice(256, 512), odd))
        ]
        for far in range(2):
            wave = parts[0] - parts[1] if far else parts[0] + parts[1]
            first = 192 * y + 384 * far
            value = grid_ref[first : first + 192, :] + wave
            for z in range(4):
                for k in range(2):
                    for f in range(2):
                        source = 48 * z + 24 * k + 12 * f
                        place = 12 * (2 * (y + 2 * far) + k)
                        out_ref[z * 2 + f, place : place + 12, :] = value[source : source + 12]


def forward_kernel(in_ref, fh_ref, fl_ref, out_ref, mix_ref):
    for s in range(16):
        north = in_ref[16 * s : 16 * s + 16, :]
        south = in_ref[16 * (31 - s) : 16 * (31 - s) + 16, :]
        for group in range(3):
            lanes = slice(128 * group, 128 * group + 128)
            mix_ref[group, 16 * s : 16 * s + 16, :] = north[:, lanes] + south[:, lanes]
            mix_ref[group, 256 + 16 * s : 256 + 16 * s + 16, :] = north[:, lanes] - south[:, lanes]
    for half in range(2):
        results = []
        for m4 in range(4):
            m = half * 4 + m4
            blocks = []
            for group in range(3):
                parts = [
                    mix_ref[group, pl.ds(base + r * 8 + m, 16, stride=16), :]
                    for base in (0, 256)
                    for r in (0, 1)
                ]
                for i in range(4):
                    blocks.append(pack([(part, i) for part in parts]))
            column = split(jnp.concatenate(blocks, axis=0))
            results.append(
                [dot3((fh_ref[m, parity], fl_ref[m, parity]), column) for parity in range(2)]
            )
        for parity in range(2):
            for r in range(2):
                tile = pack(
                    [(results[m4][parity], 2 * ((half + parity) % 2) + r) for m4 in range(4)]
                )
                for z in range(4):
                    out_ref[
                        z * 2 + half, parity * 48 : parity * 48 + 48, 128 * r : 128 * r + 128
                    ] = tile[z * 48 : z * 48 + 48]


def join_kernel(in_ref, out_ref, rows_ref):
    for parity in range(2):
        for t in range(3):
            rows = slice(parity * 48 + t * 16, parity * 48 + t * 16 + 16)
            off = 2 * t + parity
            for mr in range(8):
                lanes = slice(128 * (mr // 4), 128 * (mr // 4) + 128)
                for f in range(2):
                    rows_ref[f, pl.ds(off * 8 + mr, 16, stride=48), :] = pack(
                        [(in_ref[z * 2 + f, rows, lanes], mr % 4) for z in range(4)]
                    )
    for f in range(2):
        out_ref[:, 128 * f : 128 * f + 128] = rows_ref[f]


def part_kernel(in_ref, out_ref, rows_ref):
    for f in range(2):
        rows_ref[f] = in_ref[:, 128 * f : 128 * f + 128]
    for parity in range(2):
        for t in range(3):
            rows = slice(parity * 48 + t * 16, parity * 48 + t * 16 + 16)
            off = 2 * t + parity
            for f in range(2):
                tiles = [
                    rows_ref[f, pl.ds(off * 8 + mr, 16, stride=48), :]
                    for mr in range(8)
                ]
                for z in range(4):
                    for r in range(2):
                        out_ref[z * 2 + f, rows, 128 * r : 128 * r + 128] = pack(
                            [(tiles[4 * r + m4], z) for m4 in range(4)]
                        )


def mix_kernel(feat_ref, in_ref, own_ref, other_ref, out_ref):
    first = feat_ref[0] == 0
    for i in range(3):
        weights = []
        for r in range(2):
            own, other = own_ref[r, i], other_ref[r, i]
            weights.append(
                split(
                    jnp.concatenate(
                        [jnp.where(first, own, other), jnp.where(first, other, own)], axis=1
                    )
                )
            )
        value = in_ref[:, i]
        turned = jnp.concatenate([-value[:, 4:], value[:, :4]], axis=1)
        result = dot3(split(value.reshape(256, C)), weights[0]) + dot3(
            split(turned.reshape(256, C)), weights[1]
        )
        out_ref[:, i] = result.reshape(32, 8, C)


def inverse_kernel(in_ref, ih_ref, il_ref, out_ref, north_ref, south_ref):
    for half in range(2):
        halves = []
        for parity in range(2):
            halves.append(
                split(
                    jnp.concatenate(
                        [
                            in_ref[z * 2 + half, parity * 48 : parity * 48 + 48, :]
                            for z in range(4)
                        ],
                        axis=0,
                    )
                )
            )
        for m4 in range(4):
            m = half * 4 + m4
            even, odd = (
                dot3((ih_ref[m, parity], il_ref[m, parity]), halves[parity])
                for parity in (half, 1 - half)
            )
            for r in range(2):
                lanes = slice(128 * r, 128 * r + 128)
                a, b = even[:, lanes], odd[:, lanes]
                for value, ref in ((a + b, north_ref), (a - b, south_ref)):
                    for group in range(3):
                        ref[group, pl.ds(r * 8 + m, 16, stride=16), :] = pack(
                            [
                                (value[(4 * group + i) * 16 : (4 * group + i) * 16 + 16], m4)
                                for i in range(4)
                            ]
                        )
    for group in range(3):
        lanes = slice(128 * group, 128 * group + 128)
        out_ref[:256, lanes] = north_ref[group]
        for s in range(16):
            out_ref[16 * (31 - s) : 16 * (31 - s) + 16, lanes] = south_ref[
                group, 16 * s : 16 * s + 16, :
            ]


def points_kernel(in_ref, out_ref):
    for row in range(12):
        lanes = slice(128 * (row // 4), 128 * (row // 4) + 128)
        for f in range(2):
            tile = pack([(in_ref[z * 2 + f, :, lanes], row % 4) for z in range(4)])
            for yk in range(8):
                out_ref[
                    yk * 144 + row * 12 : yk * 144 + row * 12 + 12, 128 * f : 128 * f + 128
                ] = tile[yk * 12 : yk * 12 + 12]


def finish_kernel(south_ref, in_ref, out_ref):
    south = south_ref[0]
    for yk in range(8):
        for row in range(12):
            place = yk * 12 + jnp.where(south == 1, 11 - row, row)
            out_ref[place] = jnp.concatenate(
                [in_ref[f * 8 + yk, row * 12 : row * 12 + 12, :] for f in range(2)], axis=0
            )


def exchange(blocks, axes):
    return lax.all_to_all(blocks, axes, split_axis=0, concat_axis=0, tiled=True)


def with_halo(block, sides, width):
    for axis, dim in sides:
        count = lax.axis_size(axis)
        forward = [(i, i + 1) for i in range(count - 1)]
        backward = [(target, source) for source, target in forward]
        low = lax.ppermute(
            lax.slice_in_dim(block, block.shape[dim] - width, None, axis=dim), axis, forward
        )
        high_side = lax.ppermute(lax.slice_in_dim(block, 0, width, axis=dim), axis, backward)
        block = jnp.concatenate([low, block, high_side], axis=dim)
    return block


def partner(value):
    return lax.ppermute(value, "feat", [(0, 1), (1, 0)])


def together(*values):
    return lax.optimization_barrier(values)


def shift_out(blocks, axis):
    count = lax.axis_size(axis)
    me = lax.axis_index(axis)
    got = [lax.dynamic_index_in_dim(blocks, me, 0, keepdims=False)]
    for d in range(1, count):
        sent = lax.dynamic_index_in_dim(blocks, (me + d) % count, 0, keepdims=False)
        got.append(lax.ppermute(sent, axis, [(i, (i + d) % count) for i in range(count)]))
    return tuple(got)


def shift_in(got, axis):
    count = lax.axis_size(axis)
    me = lax.axis_index(axis)
    stacked = jnp.stack(got)
    return jnp.stack(
        [lax.dynamic_index_in_dim(stacked, (me - i) % count, 0, keepdims=False) for i in range(count)]
    )


def plane_piece(matrices):
    place = lax.axis_index(("y", "core"))
    pieces = []
    for matrix in matrices:
        rows = matrix.shape[0] // 8
        part = lax.dynamic_slice_in_dim(matrix, place * rows, rows, 0)
        pieces += [part[:, c : c + 128] for c in range(0, matrix.shape[1], 128)]
    return jnp.concatenate(pieces, axis=0)


def plane_pair(piece):
    return both(piece, lax.ppermute(piece, "core", [(0, 1), (1, 0)]), 0, "core")


def plane_gather(pair):
    return (pair,) + tuple(
        lax.ppermute(pair, "y", [(i, (i + d) % 4) for i in range(4)]) for d in range(1, 4)
    )


def plane_join(got, matrices):
    whole = shift_in(got, "y").reshape(8, -1, 128)
    joined = []
    first = 0
    for matrix in matrices:
        rows, wide = matrix.shape[0] // 8, matrix.shape[1] // 128
        part = whole[:, first : first + rows * wide].reshape(8, wide, rows, 128)
        joined.append(jnp.transpose(part, (0, 2, 1, 3)).reshape(matrix.shape))
        first += rows * wide
    return joined


def both(value, other, axis, mesh_axis="feat"):
    first = lax.axis_index(mesh_axis) == 0
    return jnp.concatenate(
        [jnp.where(first, value, other), jnp.where(first, other, value)], axis=axis
    )


def gelu(value):
    return 0.5 * value * (1.0 + lax.erf(value * math.sqrt(0.5)))


def dense(left, right):
    return jnp.dot(left, right, precision=high, preferred_element_type=F32)


def convolve(padded, depth_kernel, depth_bias, tile_rows, tile_cols):
    conv = jnp.zeros((tile_rows, tile_cols, padded.shape[2]), F32) + depth_bias
    for tap_row in range(KERNEL):
        for tap_col in range(KERNEL):
            conv = (
                conv
                + padded[tap_row : tap_row + tile_rows, tap_col : tap_col + tile_cols]
                * depth_kernel[tap_row, tap_col]
            )
    return conv


def shards(
    atmosphere,
    spectral_weight,
    mlp_in,
    mlp_out,
    ocean_state,
    depth_kernel,
    depth_bias,
    norm_gain,
    ocean_up,
    ocean_down,
    ocean_bias,
    layer_scale,
    flux_weight,
    regrid_rows,
    ocean_rows,
    land_mask,
):
    half_chan = atmosphere.shape[2]
    tile_rows, tile_cols, ocean_half = ocean_state.shape
    south = (lax.axis_index("lat") >= 2).astype(jnp.int32).reshape(1)
    feat = lax.axis_index("feat").reshape(1)
    eight = jnp.arange(8, dtype=jnp.int32)
    orders = lax.axis_index(ORDER_AXES) * 8 + eight % 4 * 2 + eight // 4
    zero = jnp.int32(0) * feat[0]

    spread = local_call(spread_kernel, shape(32, 24, 384), name="spread", smem=1)(south, atmosphere)
    spread, flat_atm, state, orders, early = together(
        spread, atmosphere.reshape(-1, half_chan), ocean_state, orders, zero
    )
    grid = exchange(spread, LON).reshape(NLON, 384)
    forward_parts = forward_matrix(early)
    tables = legendre_tables(orders)
    picked = flat_atm.at[regrid_rows.reshape(-1)].get(mode="promise_in_bounds")
    picked = jnp.moveaxis(picked.reshape(4, 4, 2, -1, half_chan), 2, 0)
    picked = shift_out(picked, "core")
    tall = with_halo(state, (("lat", 0),), KERNEL // 2)
    grid, forward_parts, tables = together(grid, forward_parts, tables)
    spectrum = local_call(fourier_kernel, shape(32, 2, 8, 384), name="fourier")(
        *forward_parts, grid
    )

    spectrum, weight, tall, picked = together(spectrum, spectral_weight, tall, picked)
    spectrum = exchange(spectrum.reshape(32, 16, 384), ORDER_AXES).reshape(512, 384)
    other_weight = partner(weight)
    picked = jnp.moveaxis(shift_in(picked, "core"), 0, 2)
    coeffs = local_call(
        forward_kernel, shape(8, 96, 256), [pltpu.VMEM((3, 512, 128), F32)], name="forward"
    )(spectrum, tables[0], tables[1])

    coeffs, other_weight, picked = together(coeffs, other_weight, picked)
    coeffs = exchange(coeffs, CHAN_AXES)
    picked = shift_out(picked, "y")
    coeffs, picked = together(coeffs, picked)
    coeffs = local_call(
        join_kernel, shape(768, 256), [pltpu.VMEM((2, 768, 128), F32)], name="join"
    )(coeffs)

    coeffs, picked = together(coeffs, shift_in(picked, "y"))
    coeffs = exchange(coeffs.reshape(32, 24, 256), ORDER_AXES).reshape(32, 3, 8, 256)
    arrived = shift_out(jnp.moveaxis(picked, 1, 0), "zh")
    mixed = local_call(mix_kernel, shape(32, 3, 8, 256), name="mix", smem=1)(
        feat, coeffs, weight, other_weight
    )

    mixed, arrived, tall = together(mixed, arrived, tall)
    mixed = exchange(mixed.reshape(32, 24, 256), ORDER_AXES).reshape(768, 256)
    arrived = jnp.moveaxis(shift_in(arrived, "zh"), 0, 1).reshape(-1, half_chan)
    other_arrived = partner(arrived)
    padded = with_halo(tall, ((LON, 1),), KERNEL // 2)
    mixed = local_call(
        part_kernel, shape(8, 96, 256), [pltpu.VMEM((2, 768, 128), F32)], name="part"
    )(mixed)

    mixed, other_arrived, late = together(mixed, other_arrived, zero)
    mixed = exchange(mixed, CHAN_AXES)
    inverse_parts = inverse_matrix(late)
    flux_rows = dense(both(arrived, other_arrived, 1), flux_weight)
    forcing = flux_rows.at[ocean_rows.reshape(-1)].get(mode="promise_in_bounds")
    conv = convolve(padded, depth_kernel, depth_bias, tile_rows, tile_cols)
    joined = conv.reshape(-1, ocean_half) + forcing
    mixed, joined, inverse_parts = together(mixed, joined, inverse_parts)
    waves = local_call(
        inverse_kernel, shape(512, 384), [pltpu.VMEM((3, 256, 128), F32)] * 2, name="inverse"
    )(mixed, tables[2], tables[3])

    waves, joined, shared = together(waves, joined, (mlp_in, mlp_out, ocean_up))
    waves = exchange(waves.reshape(32, 16, 384), ORDER_AXES).reshape(32, 2, 8, 384)
    other_joined = partner(joined)
    piece = partner(plane_piece(shared))
    summed = local_call(synthesis_kernel, shape(8, 96, 384), name="synthesis")(
        *inverse_parts, waves, grid
    )

    summed, other_joined, piece = together(summed, other_joined, piece)
    summed = exchange(summed, CHAN_AXES)
    pieces = plane_gather(plane_pair(piece))
    other_in, other_out, other_up = plane_join(pieces, shared)
    whole_up = both(ocean_up, other_up, 1)
    whole_in = both(mlp_in, other_in, 1)
    whole_out = both(mlp_out, other_out, 1)
    full_rows = both(joined, other_joined, 1)
    row_mean = jnp.mean(full_rows, axis=-1, keepdims=True)
    centered = full_rows - row_mean
    variance = jnp.mean(centered * centered, axis=-1, keepdims=True)
    normed = centered * lax.rsqrt(variance + 1e-06) * norm_gain
    update = dense(gelu(dense(normed, whole_up)), ocean_down) + ocean_bias
    mask_rows = tile_rows // BLOCK
    mask_cols = tile_cols // BLOCK
    cell_mask = (
        jnp.broadcast_to(land_mask[:, None, :, None], (mask_rows, BLOCK, mask_cols, BLOCK))
        .reshape(tile_rows, tile_cols)
        .astype(F32)
    )
    ocean_next = ocean_state + cell_mask[:, :, None] * layer_scale * update.reshape(
        tile_rows, tile_cols, ocean_half
    )
    summed, whole_in, whole_out = together(summed, whole_in, whole_out)
    points = local_call(points_kernel, shape(1152, 256), name="points")(summed)
    hidden = gelu(dense(points, whole_in))
    halves = [
        points[:, 128 * f : 128 * f + 128] + dense(hidden, whole_out[:, 128 * f : 128 * f + 128])
        for f in range(2)
    ]
    result = exchange(jnp.stack(halves).reshape(16, 144, 128), ("feat", "y", "core"))
    atmos_next = local_call(finish_kernel, shape(96, 24, 128), name="finish", smem=1)(south, result)
    return atmos_next, ocean_next


def solution(mesh):
    fine = Mesh(mesh.devices.reshape(4, 4, 4, 2, 2), ("lat", "y", "zh", "core", "feat"))
    in_specs = (
        P("lat", LON, "feat"),
        P(None, ("lat",) + LON, None, "feat"),
        P(None, "feat"),
        P(None, "feat"),
        P("lat", LON, "feat"),
        P(None, None, "feat"),
        P("feat"),
        P(),
        P(None, "feat"),
        P(None, "feat"),
        P("feat"),
        P("feat"),
        P(None, "feat"),
        P("lat", LON, None, None),
        P("lat", LON),
        P("lat", LON),
    )
    out_specs = (P("lat", LON, "feat"), P("lat", LON, "feat"))
    return jax.shard_map(shards, mesh=fine, in_specs=in_specs, out_specs=out_specs, check_vma=False)
```
